32 devices in a mesh: grp: 2 (over x), shot: 8 (over z, y), depth: 2 (over core).
Axes of the slice: x: 2, y: 2, z: 4, core: 2. Of those that a mesh axis runs over, the one named last changes fastest.
Arguments:
- wave_prev: float32 [16, 32, 128, 128], P(('grp', 'shot'), 'depth'), parts along dimension 0, may hold values from -6 to 6
- wave_now: float32 [16, 32, 128, 128], P(('grp', 'shot'), 'depth'), parts along dimension 0, may hold values from -6 to 6
- adjoint: float32 [16, 4, 32, 128, 128], P(('grp', 'shot'), None, 'depth'), parts along dimension 0, may hold values from -6 to 6
- coarse_velocity: float32 [32, 4096], P(('grp', 'depth'), 'shot'), parts along dimension 0, may hold values from 1.5 to 4.5
- filters: float32 [16, 27], replicated, may hold values from -1.25 to 1.25
- wavelet: float32 [16, 4], P(('grp', 'shot')), parts along dimension 0, may hold values from -30 to 30
- source_cell: int32 [16], P(('grp', 'shot')), parts along dimension 0, may hold values from 0 to 524287
- receiver_cells: int32 [16, 128], P(('grp', 'shot')), parts along dimension 0, may hold values from 0 to 524287
Outputs:
- gradient: float32 [32, 4096], P(('grp', 'depth'), 'shot'), parts along dimension 0
- wave_prev_out: float32 [16, 32, 128, 128], P(('grp', 'shot'), 'depth'), parts along dimension 0
- wave_now_out: float32 [16, 32, 128, 128], P(('grp', 'shot'), 'depth'), parts along dimension 0
- traces: float32 [16, 4, 128], P(('grp', 'shot')), parts along dimension 0
The draws below stay inside these ranges and needn't reach their ends.
There are 2 independent parts, one for each index of `grp`. The reference program is written for one: setup_inputs(seed, part) draws one part's arguments, and reference() takes and returns one part's arrays. A program takes and returns all parts, laid end to end along the dimension named above; an argument that names none is the same for every part. Nothing has to cross between parts.
All inputs are finite; a program needn't handle non-finite values.
Results may differ from the reference program's by a relative error of at most 0.0003.
Values sent between devices are 32-bit elements; how exact they have to be, the bound alone decides.
No kernel may reach another device: no remote copies, remote signals or barrier semaphores. Data moves between devices by JAX's collectives and lax.ppermute only.
A program may use at most 192 MiB of HBM per device.

```python
import jax
import jax.numpy as jnp
from jax import lax

NX = 128
NY = 128
STEPS = 4
CHANNELS = 16
NREC = 128
SHOTS = 8
NZ = 32
ZC = 16
XC = 64
YC = 64


def with_ends(entries, own_key, smallest, top_value):
    longest = entries.shape.index(max(entries.shape))
    spots = []
    for shift in (0, 1):
        where = [jax.random.randint(jax.random.fold_in(own_key, axis), (), 0, length) for axis, length in enumerate(entries.shape)]
        where[longest] = (where[longest] + shift) % entries.shape[longest]
        spots.append(tuple(where))
    return entries.at[spots[0]].set(smallest).at[spots[1]].set(top_value)


def block_levels(key, extent, shards, least, high):
    def one(dim, blocks):
        draws = jax.random.uniform(jax.random.fold_in(jax.random.fold_in(key, 6), dim), (blocks,), jnp.float32, least / len(shards), high / len(shards))
        return jnp.repeat(jnp.exp(draws), extent[dim] // blocks).reshape((-1,) + (1,) * (len(extent) - dim - 1))

    level = one(*shards[0])
    for cut in shards[1:]:
        level = level * one(*cut)
    return level


def gaussian(own_key, extent, width, limit, pieces=(), kind=jnp.bfloat16):
    result = jax.random.normal(own_key, extent, jnp.float32) * width
    if len(pieces) > 0:
        result = block_levels(own_key, extent, pieces, -0.22, 0.18) * result
    return jnp.clip(result, min=-limit, max=limit).astype(kind)


def setup_inputs(seed: int = 0, part: int = 0) -> dict:
    key_of = jax.random.split(jax.random.key(seed), 9)
    part_keys = jax.random.split(jax.random.fold_in(key_of[8], part), 9)
    wave_prev = gaussian(part_keys[0], (SHOTS, NZ, NX, NY), 1.0, 6.0, ((0, 8), (1, 2)), jnp.float32)
    wave_now = gaussian(part_keys[1], (SHOTS, NZ, NX, NY), 1.0, 6.0, ((0, 8), (1, 2)), jnp.float32)
    adjoint = gaussian(part_keys[2], (SHOTS, STEPS, NZ, NX, NY), 1.0, 6.0, ((0, 8), (2, 2)), jnp.float32)
    coarse_velocity = jnp.clip(1.5 + 3.0 * jax.random.uniform(part_keys[3], (ZC, XC * YC), jnp.float32) ** block_levels(part_keys[3], (ZC, XC * YC), ((0, 2), (1, 8)), -0.2, 0.2), 1.5, 4.5)
    filters = gaussian(key_of[4], (CHANNELS, 27), 27 ** -0.5, 1.25, (), jnp.float32)
    wavelet = gaussian(part_keys[5], (SHOTS, STEPS), 5.0, 30.0, ((0, 8),), jnp.float32)
    source_cell = with_ends(jax.random.randint(part_keys[6], (SHOTS,), 0, NZ * NX * NY), jax.random.fold_in(part_keys[6], 1), 0, (NZ * NX * NY) - 1).astype(jnp.int32)
    receiver_cells = with_ends(jax.random.randint(part_keys[7], (SHOTS, NREC), 0, NZ * NX * NY), jax.random.fold_in(part_keys[7], 1), 0, (NZ * NX * NY) - 1).astype(jnp.int32)
    return {"wave_prev": wave_prev, "wave_now": wave_now, "adjoint": adjoint, "coarse_velocity": coarse_velocity, "filters": filters, "wavelet": wavelet, "source_cell": source_cell, "receiver_cells": receiver_cells}


coeffs = (-205.0 / 72.0, 8.0 / 5.0, -1.0 / 5.0, 8.0 / 315.0, -1.0 / 560.0)
courant = 0.1
offsets = [(a, b, c) for a in (-1, 0, 1) for b in (-1, 0, 1) for c in (-1, 0, 1)]


def stencil(padded, row_count):
    width_x, width_y = padded.shape[1], padded.shape[2]
    lateral = jnp.pad(padded, ((0, 0), (4, 4), (4, 4)))

    def window(shift_z, shift_x, shift_y):
        return lateral[4 + shift_z:4 + shift_z + row_count, 4 + shift_x:4 + shift_x + width_x, 4 + shift_y:4 + shift_y + width_y]

    summed = 3.0 * coeffs[0] * window(0, 0, 0)
    for reach in range(1, 5):
        pairs = window(reach, 0, 0) + window(-reach, 0, 0) + window(0, reach, 0) + window(0, -reach, 0) + window(0, 0, reach) + window(0, 0, -reach)
        summed = summed + coeffs[reach] * pairs
    return summed


def upsample(coarse, half_x, half_y):
    brick_view = coarse.reshape(coarse.shape[0], half_x, half_y)
    return jnp.repeat(jnp.repeat(jnp.repeat(brick_view, 2, 0), 2, 1), 2, 2)


def coarsen(fine_field):
    depth_rows, width_x, width_y = fine_field.shape
    grouped = fine_field.reshape(depth_rows // 2, 2, width_x // 2, 2, width_y // 2, 2).sum(axis=(1, 3, 5))
    return grouped.reshape(depth_rows // 2, (width_x // 2) * (width_y // 2))


def shifted(widened, a, b, c, row_count, half_y):
    column_total = widened.shape[-1] - 2 * (half_y + 1)
    offset = half_y + 1 + b * half_y + c
    window = widened[1 + a:1 + a + row_count, offset:offset + column_total]
    column = jnp.arange(column_total, dtype=jnp.int32) % half_y
    inside = (column + c >= 0) & (column + c < half_y)
    return jnp.where(inside[None, :], window, 0.0)


def prior_scores(padded, row_count, half_y, filters):
    widened = jnp.pad(padded, ((0, 0), (half_y + 1, half_y + 1)))
    stacked = jnp.stack([shifted(widened, a, b, c, row_count, half_y) for (a, b, c) in offsets])
    scores = jnp.einsum("kt,tzn->kzn", filters, stacked, precision=lax.Precision.HIGHEST)
    return scores / (1.0 + scores * scores)


def prior_back(response_pad, row_count, half_y, filters):
    spread = jnp.einsum("kt,kzn->tzn", filters, response_pad, precision=lax.Precision.HIGHEST)
    widened = jnp.pad(spread, ((0, 0), (0, 0), (half_y + 1, half_y + 1)))
    summed = jnp.zeros((row_count, spread.shape[-1]), spread.dtype)
    for position, (a, b, c) in enumerate(offsets):
        summed = summed + shifted(widened[position], -a, -b, -c, row_count, half_y)
    return summed


def reference(wave_prev, wave_now, adjoint, coarse_velocity, filters, wavelet, source_cell, receiver_cells):
    velocity = upsample(coarse_velocity, XC, YC)
    speed_term = (courant * velocity) ** 2
    cell_index = jnp.arange(NZ * NX * NY, dtype=jnp.int32).reshape(NZ, NX, NY)

    def one_shot(inputs):
        earlier, current, adjoints, pulses, source, receivers = inputs
        source_hit = cell_index == source
        imaging = jnp.zeros_like(current)
        trace_rows = []
        for moment in range(STEPS):
            padded = jnp.pad(current, ((4, 4), (0, 0), (0, 0)))
            laplace = stencil(padded, NZ)
            following = 2.0 * current - earlier + speed_term * laplace + jnp.where(source_hit, speed_term * pulses[moment], 0.0)
            imaging = imaging + adjoints[moment] * (following - 2.0 * current + earlier)
            trace_rows.append(following.reshape(-1)[receivers])
            earlier, current = current, following
        fine_grad = -2.0 * imaging / velocity ** 3
        return earlier, current, jnp.stack(trace_rows), coarsen(fine_grad)

    last_prev, last_now, traces, shot_terms = lax.map(one_shot, (wave_prev, wave_now, adjoint, wavelet, source_cell, receiver_cells))
    image_grad = jnp.sum(shot_terms, axis=0)
    response = prior_scores(jnp.pad(coarse_velocity, ((1, 1), (0, 0))), ZC, YC, filters)
    response_pad = jnp.pad(response, ((0, 0), (1, 1), (0, 0)))
    prior_grad = prior_back(response_pad, ZC, YC, filters)
    return image_grad + prior_grad, last_prev, last_now, traces
```

```python
import functools

import jax
import jax.numpy as jnp
from jax import lax
from jax.experimental import pallas as pl
from jax.experimental.pallas import tpu as pltpu
from jax.sharding import PartitionSpec as P

SCALE = 5040.0
CENTRE = -3.0 * 14350.0
WEIGHTS = (8064.0, -1008.0, 128.0, -9.0)
REACH = 4
PAD = 8
LANES = 128
courant = 0.1
lateral_taps = [(b, e) for b in (-1, 0, 1) for e in (-1, 0, 1)]


def split(value):
    high = value.astype(jnp.bfloat16)
    low = (value - high.astype(jnp.float32)).astype(jnp.bfloat16)
    return jnp.concatenate([high, low], axis=1)


def banded(width):
    row = lax.broadcasted_iota(jnp.int32, (width, width), 0)
    column = lax.broadcasted_iota(jnp.int32, (width, width), 1)
    distance = jnp.abs(row - column)
    result = jnp.zeros((width, width), jnp.float32)
    for reach in range(1, REACH + 1):
        result = jnp.where(distance == reach, WEIGHTS[reach - 1], result)
    return jnp.concatenate([result, result], axis=0).astype(jnp.bfloat16)


def spreading(half):
    row = lax.broadcasted_iota(jnp.int32, (LANES, 2 * LANES), 0)
    column = lax.broadcasted_iota(jnp.int32, (LANES, 2 * LANES), 1)
    wanted = jnp.where(column < LANES, column // 2, half + (column - LANES) // 2)
    result = jnp.where(row == wanted, 1.0, 0.0)
    return jnp.concatenate([result, result], axis=0).astype(jnp.bfloat16)


def pairing(half, offset):
    row = lax.broadcasted_iota(jnp.int32, (LANES, LANES), 0)
    column = lax.broadcasted_iota(jnp.int32, (LANES, LANES), 1)
    result = jnp.where(row // 2 + offset == column, 1.0, 0.0)
    return jnp.concatenate([result, result], axis=0).astype(jnp.bfloat16)


def wave_kernel(
    place, source, pulses, receivers, receiver_rows, near, far, other,
    now_own, now_other, prev_own, prev_other, adjoint,
    image_out, trace_out, prev_out, now_out,
    fields, before, adjoints, last, speed, even_rows, odd_rows, imaging, pair_sum, rows_scratch, sems,
):
    shot, depth = place[0], place[1]
    steps, rows, width_x, width_y = adjoints.shape
    half_x, half_y = width_x // 2, width_y // 2
    blocks, tiles, coarse_rows = 2 * near.shape[0], near.shape[1], near.shape[2]
    half_blocks = near.shape[0]
    own_start = depth * rows
    other_start = rows - own_start

    def copies():
        inner = pl.ds(PAD, width_x)
        yield pltpu.make_async_copy(now_own, fields.at[0, pl.ds(REACH + own_start, rows), inner], sems.at[0])
        yield pltpu.make_async_copy(now_other, fields.at[0, pl.ds(REACH + other_start, rows), inner], sems.at[1])
        yield pltpu.make_async_copy(prev_own, before.at[pl.ds(own_start, rows)], sems.at[2])
        yield pltpu.make_async_copy(prev_other, before.at[pl.ds(other_start, rows)], sems.at[3])
        for moment in range(steps):
            yield pltpu.make_async_copy(adjoint.at[moment], adjoints.at[moment], sems.at[4 + moment])

    incoming = list(copies())
    for copy in incoming:
        copy.start()

    edge = depth * (2 * rows + REACH)

    def clear_sides(z, carry):
        for level in range(steps):
            fields[level, z, 0:PAD, :] = jnp.zeros((PAD, width_y), jnp.float32)
            fields[level, z, PAD + width_x : 2 * PAD + width_x, :] = jnp.zeros((PAD, width_y), jnp.float32)
        return carry

    lax.fori_loop(0, 2 * rows + 2 * REACH, clear_sides, 0)

    def clear_edge(z, carry):
        for level in range(steps):
            fields[level, edge + z] = jnp.zeros((width_x + 2 * PAD, width_y), jnp.float32)
        return carry

    lax.fori_loop(0, REACH, clear_edge, 0)

    spread = spreading(half_y)
    group = tiles * coarse_rows
    for first, slab in ((None, depth), (other, 1 - depth)):
        parts = [near[...], far[...]] if first is None else [first[...]]
        for part_number, part in enumerate(parts):
            count = part.shape[0]
            flat = part.reshape(count * group, LANES)
            fine = jnp.dot(split(flat), spread, preferred_element_type=jnp.float32)
            fine = courant * fine
            fine = fine * fine * (1.0 / SCALE)
            for position in range(count):
                target = (shot ^ (position + part_number * half_blocks)) * group
                here = pl.ds(pl.multiple_of(target, group), group)
                even_rows[here, :] = fine[position * group : (position + 1) * group, :LANES]
                odd_rows[here, :] = fine[position * group : (position + 1) * group, LANES:]
        lines = half_x // 2
        for row in range(coarse_rows):
            even = even_rows[pl.ds(row, lines, stride=coarse_rows), :]
            odd = odd_rows[pl.ds(row, lines, stride=coarse_rows), :]
            plane = slab * coarse_rows + row
            speed[plane, pl.ds(0, lines, stride=4), :] = even
            speed[plane, pl.ds(1, lines, stride=4), :] = even
            speed[plane, pl.ds(2, lines, stride=4), :] = odd
            speed[plane, pl.ds(3, lines, stride=4), :] = odd

    band = banded(width_y)
    plane_size = width_x * width_y
    source_z = source[0] // plane_size
    source_x = (source[0] % plane_size) // width_y
    source_y = source[0] % width_y
    source_mask = lax.broadcasted_iota(jnp.int32, (1, width_y), 1) == source_y
    cells = receiver_rows[...]
    cell_z = cells // plane_size
    cell_y = cells % width_y
    inside = (cell_z >= own_start) & (cell_z < own_start + rows)
    lane = lax.broadcasted_iota(jnp.int32, (cells.shape[0], width_y), 1)
    picked = (lane == cell_y) & inside

    incoming[0].wait()
    incoming[1].wait()

    half_tile = width_x // 2
    tile = 16

    def advance(moment, first_plane, own):
        for half in range(2):
            base = PAD + half * half_tile
            stacked = jnp.concatenate(
                [fields[moment, first_plane + REACH + i, base : base + half_tile, :] for i in range(4)], axis=0
            )
            along_y = jnp.dot(split(stacked), band, preferred_element_type=jnp.float32)
            for part in range(half_tile // tile):
                x = base + part * tile
                column = [fields[moment, first_plane + i, x : x + tile, :] for i in range(4 + 2 * REACH)]
                for i in range(4):
                    z = first_plane + i
                    centre = column[REACH + i]
                    total = CENTRE * centre + along_y[i * half_tile + part * tile : i * half_tile + (part + 1) * tile]
                    for reach in range(1, REACH + 1):
                        pairs = (column[REACH + i + reach] + column[REACH + i - reach]) + (
                            fields[moment, z + REACH, x + reach : x + reach + tile, :]
                            + fields[moment, z + REACH, x - reach : x - reach + tile, :]
                        )
                        total = total + WEIGHTS[reach - 1] * pairs
                    inner = slice(x - PAD, x - PAD + tile)
                    if moment == 0:
                        earlier = before[z, inner, :]
                    else:
                        earlier = fields[moment - 1, z + REACH, x : x + tile, :]
                    following = 2.0 * centre - earlier + speed[z // 2, inner, :] * total
                    if moment + 1 < steps:
                        fields[moment + 1, z + REACH, x : x + tile, :] = following
                    else:
                        last[z - own_start, inner, :] = following
                    if own:
                        own_z = z - own_start
                        term = adjoints[moment, own_z, inner, :] * total
                        if moment == 0:
                            imaging[own_z, inner, :] = term
                        else:
                            imaging[own_z, inner, :] += term

    outgoing = [
        pltpu.make_async_copy(
            fields.at[steps - 1, pl.ds(REACH + own_start, rows), pl.ds(PAD, width_x)], prev_out, sems.at[4 + steps]
        ),
        pltpu.make_async_copy(last, now_out, sems.at[5 + steps]),
    ]

    for moment in range(steps):
        if moment == 0:
            incoming[2].wait()
            incoming[3].wait()
        incoming[4 + moment].wait()

        def own_group(index, carry):
            advance(moment, own_start + 4 * index, True)
            return carry

        lax.fori_loop(0, rows // 4, own_group, 0)
        extra = REACH * (steps - 1 - moment)
        halo_start = jnp.where(depth == 0, rows, rows - extra)

        def halo_group(index, carry):
            advance(moment, halo_start + 4 * index, False)
            return carry

        if extra > 0:
            lax.fori_loop(0, extra // 4, halo_group, 0)

        low = own_start - depth * extra
        amount = SCALE * pulses[0, moment]

        @pl.when((source_z >= low) & (source_z < low + rows + extra))
        def _():
            bump = jnp.where(source_mask, speed[source_z // 2, pl.ds(source_x, 1), :] * amount, 0.0)
            if moment + 1 < steps:
                fields[moment + 1, source_z + REACH, pl.ds(source_x + PAD, 1), :] += bump
            else:
                last[source_z - own_start, pl.ds(source_x, 1), :] += bump

        @pl.when((source_z >= own_start) & (source_z < own_start + rows))
        def _():
            own_z = source_z - own_start
            weight = adjoints[moment, own_z, pl.ds(source_x, 1), :]
            imaging[own_z, pl.ds(source_x, 1), :] += jnp.where(source_mask, weight * amount, 0.0)

        if moment >= steps - 2:
            outgoing[moment - steps + 2].start()

        def fetch(index, carry):
            for lane_number in range(8):
                number = index * 8 + lane_number
                cell = receivers[0, number]
                z = jnp.clip(cell // plane_size, own_start, own_start + rows - 1)
                x = (cell % plane_size) // width_y
                if moment + 1 < steps:
                    line = fields[moment + 1, z + REACH, pl.ds(x + PAD, 1), :]
                else:
                    line = last[z - own_start, pl.ds(x, 1), :]
                rows_scratch[pl.ds(number, 1), :] = line
            return carry

        lax.fori_loop(0, receivers.shape[1] // 8, fetch, 0)
        values = jnp.where(picked, rows_scratch[...], 0.0)
        line = lax.dot_general(
            jnp.ones((8, width_y), jnp.float32), values, (((1,), (1,)), ((), ())),
            precision=lax.Precision.HIGHEST, preferred_element_type=jnp.float32,
        )
        trace_out[moment : moment + 1, :] = line[0:1, :]

    gather = jnp.concatenate([pairing(half_y, 0), pairing(half_y, half_y)], axis=0)
    lines = half_x // 2
    for row in range(coarse_rows):
        pair_sum[...] = imaging[2 * row] + imaging[2 * row + 1]
        even = pair_sum[pl.ds(0, lines, stride=4), :] + pair_sum[pl.ds(1, lines, stride=4), :]
        odd = pair_sum[pl.ds(2, lines, stride=4), :] + pair_sum[pl.ds(3, lines, stride=4), :]
        coarse = jnp.dot(
            jnp.concatenate([split(even), split(odd)], axis=1), gather, preferred_element_type=jnp.float32
        )
        even_rows[pl.ds(row, lines, stride=coarse_rows), :] = coarse
    for position in range(blocks):
        origin = pl.ds(pl.multiple_of((shot ^ position) * group, group), group)
        image_out[position] = even_rows[origin, :].reshape(tiles, coarse_rows, LANES)

    for copy in outgoing:
        copy.wait()


def prior_kernel(place, filters, near, far, other, prior_out, joined, rolled, shifts, responses):
    shot, depth = place[0], place[1]
    half_blocks, tiles, coarse_rows = near.shape[0], near.shape[1], near.shape[2]
    shots = 2 * half_blocks
    half_y = LANES // 2
    channels = filters.shape[0]
    wide = tiles + 2
    total_tiles = shots * tiles
    inner_rows = (coarse_rows + 2) * wide
    padded_rows = -(-inner_rows // 8) * 8
    own_rows = coarse_rows * wide
    height = shifts.shape[1]
    lane = lax.broadcasted_iota(jnp.int32, (1, LANES), 1)
    column = lane % half_y

    joined[...] = jnp.zeros_like(joined)
    rolled[...] = jnp.zeros_like(rolled)
    for j in range(wide):
        absolute = shot * tiles - 1 + j
        exists = (absolute >= 0) & (absolute < total_tiles)
        safe = jnp.clip(absolute, 0, total_tiles - 1)
        position = shot ^ (safe // tiles)
        which = safe % tiles

        @pl.when(exists & (position < half_blocks))
        def _():
            joined[pl.ds(2 * wide + j, coarse_rows, stride=wide), :] = near[position, which]

        @pl.when(exists & (position >= half_blocks))
        def _():
            joined[pl.ds(2 * wide + j, coarse_rows, stride=wide), :] = far[position - half_blocks, which]

        @pl.when(exists & (depth == 1))
        def _():
            tile = other[position, which]
            joined[pl.ds(j, 1), :] = tile[coarse_rows - 2 : coarse_rows - 1]
            joined[pl.ds(wide + j, 1), :] = tile[coarse_rows - 1 : coarse_rows]

        @pl.when(exists & (depth == 0))
        def _():
            tile = other[position, which]
            joined[pl.ds((coarse_rows + 2) * wide + j, 1), :] = tile[0:1]
            joined[pl.ds((coarse_rows + 3) * wide + j, 1), :] = tile[1:2]

    def shifted(value, b, e):
        count = value.shape[0]
        offset = b * half_y + e
        if offset == 0:
            return value
        turned = pltpu.roll(value, (-offset) % LANES, 1)
        rolled[8 : 8 + count, :] = turned
        if offset > 0:
            moved = jnp.where(lane < LANES - offset, turned, rolled[9 : 9 + count, :])
        else:
            moved = jnp.where(lane >= -offset, turned, rolled[7 : 7 + count, :])
        if e != 0:
            moved = jnp.where((column + e >= 0) & (column + e < half_y), moved, 0.0)
        return moved

    whole = joined[...]
    for number, (b, e) in enumerate(lateral_taps):
        shifts[number] = shifted(whole, b, e)

    row = lax.broadcasted_iota(jnp.int32, (padded_rows, LANES), 0)
    valid = row < inner_rows
    valid = valid & ((row >= wide) | (depth != 0))
    valid = valid & ((row < (coarse_rows + 1) * wide) | (depth != 1))
    first_tile = row == 0
    last_tile = row == wide - 1
    for z in range(1, coarse_rows + 2):
        first_tile = first_tile | (row == z * wide)
        last_tile = last_tile | (row == z * wide + wide - 1)
    valid = valid & jnp.logical_not(first_tile & (shot == 0))
    valid = valid & jnp.logical_not(last_tile & (shot == shots - 1))
    keep = jnp.where(valid, 1.0, 0.0)

    def forward(index, carry):
        scores = [jnp.zeros((padded_rows, LANES), jnp.float32) for _ in range(4)]
        for a in (-1, 0, 1):
            for number in range(9):
                value = shifts[number, (1 + a) * wide : (1 + a) * wide + padded_rows, :]
                tap = (a + 1) * 9 + number
                for k in range(4):
                    scores[k] = scores[k] + filters[index * 4 + k, tap] * value
        for k in range(4):
            answer = scores[k] / (1.0 + scores[k] * scores[k])
            responses[index * 4 + k, 0:padded_rows, :] = jnp.where(keep > 0.0, answer, 0.0)
        return carry

    lax.fori_loop(0, channels // 4, forward, 0)

    result = jnp.zeros((own_rows, LANES), jnp.float32)
    for chosen in ((0, 1, 2), (3, 4, 5), (6, 7, 8)):

        def backward(k, sums):
            sums = list(sums)
            for a in (-1, 0, 1):
                value = responses[k, (1 - a) * wide : (1 - a) * wide + own_rows, :]
                for spot, number in enumerate(chosen):
                    sums[spot] = sums[spot] + filters[k, (a + 1) * 9 + number] * value
            return tuple(sums)

        sums = lax.fori_loop(
            0, channels, backward, tuple(jnp.zeros((own_rows, LANES), jnp.float32) for _ in chosen)
        )
        for spot, number in enumerate(chosen):
            b, e = lateral_taps[number]
            result = result + shifted(sums[spot], -b, -e)
    joined[0:own_rows, :] = result
    for j in range(tiles):
        prior_out[j] = joined[pl.ds(1 + j, coarse_rows, stride=wide), :]


def xor_pairs(count, bit):
    return [(i, i ^ bit) for i in range(count)]


def body(
    wave_prev, wave_now, adjoint, coarse_velocity, filters, wavelet, source_cell, receiver_cells
):
    f32 = jnp.float32
    steps, rows, width_x, width_y = adjoint.shape[1:]
    shots = lax.axis_size("shot")
    coarse_rows, columns = coarse_velocity.shape
    tiles = columns // LANES
    receiver_count = receiver_cells.shape[1]
    assert lax.axis_size("depth") == 2 and shots & (shots - 1) == 0 and shots > 1
    assert width_y == LANES and width_x % 64 == 0 and tiles * LANES == columns
    assert rows % 4 == 0 and rows >= REACH * steps and coarse_rows * 2 == rows and coarse_rows % 8 == 0
    assert receiver_count % 8 == 0 and filters.shape[0] % 4 == 0

    swap = [(0, 1), (1, 0)]
    now_other = lax.ppermute(wave_now, "depth", swap)
    prev_other = lax.ppermute(wave_prev, "depth", swap)

    block = coarse_velocity.reshape(coarse_rows, tiles, LANES).transpose(1, 0, 2)
    near = block[None]
    bit = 1
    while 2 * bit < shots:
        near = jnp.concatenate([near, lax.ppermute(near, "shot", xor_pairs(shots, bit))], axis=0)
        bit *= 2
    far = lax.ppermute(near, "shot", xor_pairs(shots, bit))
    other = lax.ppermute(jnp.concatenate([near, far], axis=0), "depth", swap)

    shot, depth = lax.axis_index("shot"), lax.axis_index("depth")
    place = jnp.stack([shot, depth]).astype(jnp.int32)
    smem = pl.BlockSpec(memory_space=pltpu.SMEM)
    vmem = pl.BlockSpec(memory_space=pltpu.VMEM)
    hbm = pl.BlockSpec(memory_space=pl.ANY)
    depth_planes = 2 * rows + 2 * REACH
    image, trace, prev_out, now_out = pl.pallas_call(
        wave_kernel,
        out_shape=(
            jax.ShapeDtypeStruct((shots, tiles, coarse_rows, LANES), f32),
            jax.ShapeDtypeStruct((steps, receiver_count), f32),
            jax.ShapeDtypeStruct((rows, width_x, width_y), f32),
            jax.ShapeDtypeStruct((rows, width_x, width_y), f32),
        ),
        in_specs=[smem] * 4 + [vmem] * 4 + [hbm] * 5,
        out_specs=(vmem, vmem, hbm, hbm),
        scratch_shapes=[
            pltpu.VMEM((steps, depth_planes, width_x + 2 * PAD, width_y), f32),
            pltpu.VMEM((2 * rows, width_x, width_y), f32),
            pltpu.VMEM((steps, rows, width_x, width_y), f32),
            pltpu.VMEM((rows, width_x, width_y), f32),
            pltpu.VMEM((2 * coarse_rows, width_x, width_y), f32),
            pltpu.VMEM((shots * tiles * coarse_rows, LANES), f32),
            pltpu.VMEM((shots * tiles * coarse_rows, LANES), f32),
            pltpu.VMEM((rows, width_x, width_y), f32),
            pltpu.VMEM((width_x, width_y), f32),
            pltpu.VMEM((receiver_count, width_y), f32),
            pltpu.SemaphoreType.DMA((6 + steps,)),
        ],
        cost_estimate=pl.CostEstimate(flops=200_000_000, bytes_accessed=12_000_000, transcendentals=0),
        compiler_params=pltpu.CompilerParams(vmem_limit_bytes=48 * 1024 * 1024),
        name="wave",
    )(
        place, source_cell, wavelet, receiver_cells, receiver_cells.reshape(receiver_count, 1), near, far, other,
        wave_now[0], now_other[0], wave_prev[0], prev_other[0], adjoint[0],
    )

    wide = tiles + 2
    total_rows = (coarse_rows + 4) * wide
    height = -(-total_rows // 8) * 8 + 8
    response_rows = -(-(coarse_rows + 2) * wide // 8) * 8
    prior = pl.pallas_call(
        prior_kernel,
        out_shape=jax.ShapeDtypeStruct((tiles, coarse_rows, LANES), f32),
        in_specs=[smem, smem, vmem, vmem, vmem],
        out_specs=vmem,
        scratch_shapes=[
            pltpu.VMEM((height, LANES), f32),
            pltpu.VMEM((height + 16, LANES), f32),
            pltpu.VMEM((9, height, LANES), f32),
            pltpu.VMEM((filters.shape[0], response_rows, LANES), f32),
        ],
        cost_estimate=pl.CostEstimate(flops=10_000_000, bytes_accessed=1_000_000, transcendentals=0),
        name="prior",
    )(place, filters, near, far, other)

    trace_other = lax.ppermute(trace, "depth", swap)
    kept = image
    while bit > 0:
        arrived = lax.ppermute(kept[bit:], "shot", xor_pairs(shots, bit))
        kept = kept[:bit] + arrived
        bit //= 2
    share = kept[0] * ((-2.0 * courant * courant / SCALE) / block) + prior
    gradient = share.transpose(1, 0, 2).reshape(coarse_rows, columns)
    return gradient, prev_out[None], now_out[None], (trace + trace_other)[None]


def solution(mesh):
    return jax.shard_map(
        body,
        mesh=mesh,
        in_specs=(
            P(("grp", "shot"), "depth", None, None),
            P(("grp", "shot"), "depth", None, None),
            P(("grp", "shot"), None, "depth", None, None),
            P(("grp", "depth"), "shot"),
            P(),
            P(("grp", "shot"), None),
            P(("grp", "shot")),
            P(("grp", "shot"), None),
        ),
        out_specs=(
            P(("grp", "depth"), "shot"),
            P(("grp", "shot"), "depth", None, None),
            P(("grp", "shot"), "depth", None, None),
            P(("grp", "shot"), None, None),
        ),
        check_vma=False,
    )
```

```python
import functools

import jax
import jax.numpy as jnp
from jax import lax
from jax.experimental import pallas as pl
from jax.experimental.pallas import tpu as pltpu
from jax.sharding import PartitionSpec as P


SCALE = 5040.0
CENTRE = -3.0 * 14350.0
WEIGHTS = (8064.0, -1008.0, 128.0, -9.0)
REACH = 4
PAD = 8
LANES = 128
TILE = 16
GRANT = 32 * 1024 * 1024
courant = 0.1
lateral_taps = [(b, e) for b in (-1, 0, 1) for e in (-1, 0, 1)]


def split(value):
    high = value.astype(jnp.bfloat16)
    low = (value - high.astype(jnp.float32)).astype(jnp.bfloat16)
    return jnp.concatenate([high, low], axis=1)


def banded(width):
    row = lax.broadcasted_iota(jnp.int32, (width, width), 0)
    column = lax.broadcasted_iota(jnp.int32, (width, width), 1)
    distance = jnp.abs(row - column)
    result = jnp.zeros((width, width), jnp.float32)
    for reach in range(1, REACH + 1):
        result = jnp.where(distance == reach, WEIGHTS[reach - 1], result)
    return jnp.concatenate([result, result], axis=0).astype(jnp.bfloat16)


def spreading(half):
    row = lax.broadcasted_iota(jnp.int32, (LANES, 2 * LANES), 0)
    column = lax.broadcasted_iota(jnp.int32, (LANES, 2 * LANES), 1)
    wanted = jnp.where(column < LANES, column // 2, half + (column - LANES) // 2)
    result = jnp.where(row == wanted, 1.0, 0.0)
    return jnp.concatenate([result, result], axis=0).astype(jnp.bfloat16)


def pairing(offset):
    row = lax.broadcasted_iota(jnp.int32, (LANES, LANES), 0)
    column = lax.broadcasted_iota(jnp.int32, (LANES, LANES), 1)
    result = jnp.where(row // 2 + offset == column, 1.0, 0.0)
    return jnp.concatenate([result, result], axis=0).astype(jnp.bfloat16)


def find(cell, width_x, width_y):
    plane = width_x * width_y
    return lax.div(cell[0], plane), lax.div(lax.rem(cell[0], plane), width_y), lax.rem(cell[0], width_y)


def stencil_group(planes, first, x, band, use):
    stacked = jnp.concatenate([planes[first + REACH + i, x : x + TILE, :] for i in range(4)], axis=0)
    along_y = jnp.dot(split(stacked), band, preferred_element_type=jnp.float32)
    column = [planes[first + i, x : x + TILE, :] for i in range(4 + 2 * REACH)]
    for i in range(4):
        centre = column[REACH + i]
        total = CENTRE * centre + along_y[i * TILE : (i + 1) * TILE]
        for reach in range(1, REACH + 1):
            pairs = (column[REACH + i + reach] + column[REACH + i - reach]) + (
                planes[first + REACH + i, x + reach : x + reach + TILE, :]
                + planes[first + REACH + i, x - reach : x - reach + TILE, :]
            )
            total = total + WEIGHTS[reach - 1] * pairs
        use(i, slice(x - PAD, x - PAD + TILE), centre, total)


def clear_sides(planes, count, width_x, width_y):
    def step(z, carry):
        planes[z, 0:PAD, :] = jnp.zeros((PAD, width_y), jnp.float32)
        planes[z, PAD + width_x : 2 * PAD + width_x, :] = jnp.zeros((PAD, width_y), jnp.float32)
        return carry

    lax.fori_loop(0, count, step, 0)


def first_steps(planes, laplace, base, offset, target, earlier, earlier_first, band):
    for part in range((planes.shape[1] - 2 * PAD) // TILE):

        def use(i, inner, centre, total):
            laplace[target + i, inner, :] = total
            base[target + i, inner, :] = 2.0 * centre - earlier[earlier_first + i, inner, :]

        stencil_group(planes, offset, PAD + part * TILE, band, use)


def inner_kernel(place, now_own, prev_own, block, laplace, base, block_out, planes, earlier, field_sems, sems):
    depth = place[1]
    rows, width_x, width_y = now_own.shape
    chunks = rows // 4
    fields = [
        pltpu.make_async_copy(
            now_own.at[pl.ds(4 * chunk, 4)], planes.at[pl.ds(REACH + 4 * chunk, 4), pl.ds(PAD, width_x)],
            field_sems.at[chunk],
        )
        for chunk in range(chunks)
    ]
    befores = [
        pltpu.make_async_copy(
            prev_own.at[pl.ds(depth * REACH + 4 * index, 4)], earlier.at[pl.ds(4 * index, 4)], sems.at[index]
        )
        for index in range(chunks - 1)
    ]
    own_block = pltpu.make_async_copy(block, block_out, sems.at[chunks - 1])
    for copy in (*fields[:3], befores[0], *fields[3:], *befores[1:], own_block):
        copy.start()
    clear_sides(planes, rows + 2 * REACH, width_x, width_y)
    edge = depth * (rows + REACH)
    for z in range(REACH):
        planes[edge + z] = jnp.zeros((width_x + 2 * PAD, width_y), jnp.float32)
    band = banded(width_y)
    for chunk in range(2):
        fields[chunk].wait()

    def group(index, carry):
        pltpu.make_async_copy(
            now_own.at[pl.ds(0, 4)], planes.at[pl.ds(0, 4), pl.ds(PAD, width_x)], field_sems.at[index + 2]
        ).wait()
        pltpu.make_async_copy(prev_own.at[pl.ds(0, 4)], earlier.at[pl.ds(0, 4)], sems.at[index]).wait()
        first_steps(planes, laplace, base, depth * REACH + 4 * index, 4 * index, earlier, 4 * index, band)
        return carry

    lax.fori_loop(0, chunks - 2, group, 0)
    befores[chunks - 2].wait()
    last = 4 * (chunks - 2)
    first_steps(planes, laplace, base, depth * REACH + last, last, earlier, last, band)
    own_block.wait()


def outer_kernel(
    place, now_own, now_other, prev_own, prev_other, laplace, base, planes, earlier, field_sems, sems,
):
    depth = place[1]
    rows, width_x, width_y = now_own.shape
    extent = laplace.shape[0] - REACH
    near_count = 2 * REACH
    chunks = rows // 4
    inner = pl.ds(PAD, width_x)
    own_row = (1 - depth) * (rows - REACH)

    def ordered(index, count):
        return index + depth * (count - 1 - 2 * index)

    own = pltpu.make_async_copy(
        now_own.at[pl.ds((1 - depth) * (rows - near_count), near_count)],
        planes.at[pl.ds(depth * rows, near_count), inner], field_sems.at[chunks],
    )
    others = [
        pltpu.make_async_copy(
            now_other.at[pl.ds(4 * ordered(chunk, chunks), 4)],
            planes.at[pl.ds((1 - depth) * near_count + 4 * ordered(chunk, chunks), 4), inner], field_sems.at[chunk],
        )
        for chunk in range(chunks)
    ]
    own_before = pltpu.make_async_copy(
        prev_own.at[pl.ds(own_row, REACH)], earlier.at[pl.ds(0, REACH)], sems.at[0]
    )
    before = pltpu.make_async_copy(
        prev_other.at[pl.ds(depth * (rows - extent), extent)], earlier.at[pl.ds(REACH, extent)], sems.at[1]
    )
    for copy in (own, others[0], own_before, others[1], before, *others[2:]):
        copy.start()
    clear_sides(planes, rows + near_count, width_x, width_y)
    band = banded(width_y)
    for copy in (own, others[0], own_before):
        copy.wait()

    first_steps(planes, laplace, base, depth * extent, 0, earlier, 0, band)
    before.wait()

    def group(index, carry):
        pltpu.make_async_copy(
            now_other.at[pl.ds(0, 4)], planes.at[pl.ds(0, 4), inner], field_sems.at[index + 1]
        ).wait()
        step = 4 * ordered(index, extent // 4)
        first_steps(planes, laplace, base, (1 - depth) * 4 + step, REACH + step, earlier, REACH + step, band)
        return carry

    lax.fori_loop(0, extent // 4, group, 0)
    for chunk in range(extent // 4 + 1, chunks):
        others[chunk].wait()


def wave_kernel(
    place, source, pulses, receivers, near, far, other_near, other_far,
    laplace_in, base_in, laplace_beyond, base_beyond, now_own, now_other, adjoint,
    image_out, lines_out, prev_out, now_out,
    fields, adjoints, last, start, speed, even_rows, odd_rows, imaging, pair_sum, sems,
):
    shot, depth = place[0], place[1]
    steps, rows, width_x, width_y = adjoints.shape
    half_x, half_y = width_x // 2, width_y // 2
    blocks, tiles, coarse_rows = 2 * near.shape[0], near.shape[1], near.shape[2]
    half_blocks = near.shape[0]
    own_start = depth * rows

    extent = REACH * (steps - 1)
    starts = [
        pltpu.make_async_copy(now_own, start.at[pl.ds(depth * extent, rows)], sems.at[steps]),
        pltpu.make_async_copy(
            now_other.at[pl.ds(depth * (rows - extent), extent)], start.at[pl.ds((1 - depth) * rows, extent)],
            sems.at[steps + 1],
        ),
    ]
    incoming = [
        pltpu.make_async_copy(adjoint.at[moment], adjoints.at[moment], sems.at[moment]) for moment in range(steps)
    ]
    for copy in (incoming[0], *starts, *incoming[1:]):
        copy.start()
    source_z, source_x, source_y = find(source, width_x, width_y)
    source_mask = lax.broadcasted_iota(jnp.int32, (1, width_y), 1) == source_y

    edge = depth * (2 * rows + REACH)
    for level in range(steps - 1):
        clear_sides(fields.at[level], 2 * rows + 2 * REACH, width_x, width_y)

    def clear_edge(z, carry):
        for level in range(steps - 1):
            fields[level, edge + z] = jnp.zeros((width_x + 2 * PAD, width_y), jnp.float32)
        return carry

    lax.fori_loop(0, REACH, clear_edge, 0)

    spread = spreading(half_y)
    group = tiles * coarse_rows
    lines = half_x // 2
    for parts, slab in (((near, far), depth), ((other_near, other_far), 1 - depth)):
        for part_number, part in enumerate(parts):
            flat = part[...].reshape(half_blocks * group, LANES)
            fine = jnp.dot(split(flat), spread, preferred_element_type=jnp.float32)
            fine = courant * fine
            fine = fine * fine * (1.0 / SCALE)
            for position in range(half_blocks):
                target = (shot ^ (position + part_number * half_blocks)) * group
                here = pl.ds(pl.multiple_of(target, group), group)
                even_rows[here, :] = fine[position * group : (position + 1) * group, :LANES]
                odd_rows[here, :] = fine[position * group : (position + 1) * group, LANES:]
        for row in range(coarse_rows):
            even = even_rows[pl.ds(row, lines, stride=coarse_rows), :]
            odd = odd_rows[pl.ds(row, lines, stride=coarse_rows), :]
            plane = slab * coarse_rows + row
            speed[plane, pl.ds(0, lines, stride=4), :] = even
            speed[plane, pl.ds(1, lines, stride=4), :] = even
            speed[plane, pl.ds(2, lines, stride=4), :] = odd
            speed[plane, pl.ds(3, lines, stride=4), :] = odd

    band = banded(width_y)
    outgoing = [
        pltpu.make_async_copy(
            fields.at[steps - 2, pl.ds(REACH + own_start, rows), pl.ds(PAD, width_x)], prev_out, sems.at[steps + 2]
        ),
        pltpu.make_async_copy(last, now_out, sems.at[steps + 3]),
    ]

    for moment in range(steps):
        extra = REACH * (steps - 1 - moment)
        level = moment - 1

        def advance(z0, own):
            for part in range(width_x // TILE):

                def use(i, inner, centre, total):
                    z = z0 + i
                    wide = slice(inner.start + PAD, inner.stop + PAD)
                    if moment == 1:
                        before = start[z - depth * (rows - extent), inner, :]
                    else:
                        before = fields[level - 1, z + REACH, wide, :]
                    following = 2.0 * centre - before + speed[z // 2, inner, :] * total
                    if moment + 1 < steps:
                        fields[level + 1, z + REACH, wide, :] = following
                    else:
                        last[z - own_start, inner, :] = following
                    if own:
                        own_z = z - own_start
                        imaging[own_z, inner, :] += adjoints[moment, own_z, inner, :] * total

                stencil_group(fields.at[level], z0, PAD + part * TILE, band, use)

        incoming[moment].wait()
        if moment == 0:

            def begin(first, laplace, base, offset, own):
                def plane(index, carry):
                    z = first + index
                    total = laplace[offset + index]
                    fields[0, z + REACH, PAD : PAD + width_x, :] = base[offset + index] + speed[z // 2] * total
                    if own:
                        imaging[z - own_start] = adjoints[0, z - own_start] * total
                    return carry

                return plane

            inside = rows - REACH
            lax.fori_loop(0, inside, begin(own_start + depth * REACH, laplace_in, base_in, 0, True), 0)
            next_start = own_start + (1 - depth) * inside
            lax.fori_loop(0, REACH, begin(next_start, laplace_beyond, base_beyond, 0, True), 0)
            beyond_start = rows - depth * extent
            lax.fori_loop(0, extent, begin(beyond_start, laplace_beyond, base_beyond, REACH, False), 0)
        else:
            if moment == 1:
                for copy in starts:
                    copy.wait()

            def own_group(index, carry):
                advance(own_start + 4 * index, True)
                return carry

            def other_group(index, carry):
                advance(jnp.where(depth == 0, rows, rows - extra) + 4 * index, False)
                return carry

            lax.fori_loop(0, rows // 4, own_group, 0)
            if extra > 0:
                lax.fori_loop(0, extra // 4, other_group, 0)

        low = own_start - depth * extra
        amount = SCALE * pulses[0, moment]

        @pl.when((source_z >= low) & (source_z < low + rows + extra))
        def _():
            bump = jnp.where(source_mask, speed[source_z // 2, pl.ds(source_x, 1), :] * amount, 0.0)
            if moment + 1 < steps:
                fields[moment, source_z + REACH, pl.ds(source_x + PAD, 1), :] += bump
            else:
                last[source_z - own_start, pl.ds(source_x, 1), :] += bump

        @pl.when((source_z >= own_start) & (source_z < own_start + rows))
        def _():
            own_z = source_z - own_start
            weight = adjoints[moment, own_z, pl.ds(source_x, 1), :] * amount
            imaging[own_z, pl.ds(source_x, 1), :] += jnp.where(source_mask, weight, 0.0)

        if moment >= steps - 2:
            outgoing[moment - steps + 2].start()

    gather = jnp.concatenate([pairing(0), pairing(half_y)], axis=0)
    for row in range(coarse_rows):
        pair_sum[...] = imaging[2 * row] + imaging[2 * row + 1]
        even = pair_sum[pl.ds(0, lines, stride=4), :] + pair_sum[pl.ds(1, lines, stride=4), :]
        odd = pair_sum[pl.ds(2, lines, stride=4), :] + pair_sum[pl.ds(3, lines, stride=4), :]
        coarse = jnp.dot(
            jnp.concatenate([split(even), split(odd)], axis=1), gather, preferred_element_type=jnp.float32
        )
        even_rows[pl.ds(row, lines, stride=coarse_rows), :] = coarse
    for position in range(blocks):
        origin = pl.ds(pl.multiple_of((shot ^ position) * group, group), group)
        image_out[position] = even_rows[origin, :].reshape(tiles, coarse_rows, LANES)

    def fetch(index, carry):
        for offset in range(8):
            number = index * 8 + offset
            z, x = receivers[0, number], receivers[1, number]
            for moment in range(steps - 1):
                lines_out[moment, pl.ds(number, 1), :] = fields[moment, own_start + z + REACH, pl.ds(x + PAD, 1), :]
            lines_out[steps - 1, pl.ds(number, 1), :] = last[z, pl.ds(x, 1), :]
        return carry

    lax.fori_loop(0, receivers.shape[1] // 8, fetch, 0)

    for copy in outgoing:
        copy.wait()


def lateral_shift(rolled, value, b, e, half_y):
    lane = lax.broadcasted_iota(jnp.int32, (1, LANES), 1)
    column = lane % half_y
    count = value.shape[0]
    offset = b * half_y + e
    if offset == 0:
        return value
    turned = pltpu.roll(value, (-offset) % LANES, 1)
    rolled[8 : 8 + count, :] = turned
    if offset > 0:
        moved = jnp.where(lane < LANES - offset, turned, rolled[9 : 9 + count, :])
    else:
        moved = jnp.where(lane >= -offset, turned, rolled[7 : 7 + count, :])
    if e != 0:
        moved = jnp.where((column + e >= 0) & (column + e < half_y), moved, 0.0)
    return moved


def response_kernel(place, filters, near, far, other_near, other_far, responses, joined, rolled, shifts):
    shot, depth = place[0], place[1]
    half_blocks, tiles, coarse_rows = near.shape[0], near.shape[1], near.shape[2]
    shots = 2 * half_blocks
    half_y = LANES // 2
    channels = filters.shape[0]
    wide = tiles + 2
    total_tiles = shots * tiles
    inner_rows = (coarse_rows + 2) * wide
    padded_rows = responses.shape[1]

    joined[...] = jnp.zeros_like(joined)
    rolled[...] = jnp.zeros_like(rolled)
    for j in range(wide):
        absolute = shot * tiles - 1 + j
        exists = (absolute >= 0) & (absolute < total_tiles)
        safe = jnp.clip(absolute, 0, total_tiles - 1)
        position = shot ^ lax.div(safe, tiles)
        which = lax.rem(safe, tiles)
        for own_part, other_part, chosen, start in (
            (near, other_near, position < half_blocks, 0), (far, other_far, position >= half_blocks, half_blocks)
        ):

            @pl.when(exists & chosen)
            def _():
                joined[pl.ds(2 * wide + j, coarse_rows, stride=wide), :] = own_part[position - start, which]
                tile = other_part[position - start, which]

                @pl.when(depth == 1)
                def _():
                    joined[pl.ds(j, 1), :] = tile[coarse_rows - 2 : coarse_rows - 1]
                    joined[pl.ds(wide + j, 1), :] = tile[coarse_rows - 1 : coarse_rows]

                @pl.when(depth == 0)
                def _():
                    joined[pl.ds((coarse_rows + 2) * wide + j, 1), :] = tile[0:1]
                    joined[pl.ds((coarse_rows + 3) * wide + j, 1), :] = tile[1:2]

    whole = joined[...]
    for number, (b, e) in enumerate(lateral_taps):
        shifts[number] = lateral_shift(rolled, whole, b, e, half_y)

    row = lax.broadcasted_iota(jnp.int32, (padded_rows, LANES), 0)
    valid = row < inner_rows
    valid = valid & ((row >= wide) | (depth != 0))
    valid = valid & ((row < (coarse_rows + 1) * wide) | (depth != 1))
    first_tile = row == 0
    last_tile = row == wide - 1
    for z in range(1, coarse_rows + 2):
        first_tile = first_tile | (row == z * wide)
        last_tile = last_tile | (row == z * wide + wide - 1)
    valid = valid & jnp.logical_not(first_tile & (shot == 0))
    valid = valid & jnp.logical_not(last_tile & (shot == shots - 1))
    keep = jnp.where(valid, 1.0, 0.0)

    def forward(index, carry):
        scores = [jnp.zeros((padded_rows, LANES), jnp.float32) for _ in range(4)]
        for a in (-1, 0, 1):
            for number in range(9):
                value = shifts[number, (1 + a) * wide : (1 + a) * wide + padded_rows, :]
                tap = (a + 1) * 9 + number
                for k in range(4):
                    scores[k] = scores[k] + filters[index * 4 + k, tap] * value
        for k in range(4):
            answer = scores[k] / (1.0 + scores[k] * scores[k])
            responses[index * 4 + k] = jnp.where(keep > 0.0, answer, 0.0)
        return carry

    lax.fori_loop(0, channels // 4, forward, 0)


def prior_kernel(
    shape, place, filters, responses, cells, lines, prior_out, trace_out, joined, rolled
):
    rows, width_x, width_y, coarse_rows, tiles = shape
    depth = place[1]
    half_y = LANES // 2
    channels = filters.shape[0]
    wide = tiles + 2
    own_rows = coarse_rows * wide
    rolled[...] = jnp.zeros_like(rolled)
    result = jnp.zeros((own_rows, LANES), jnp.float32)
    for chosen in ((0, 1, 2, 3, 4), (5, 6, 7, 8)):

        def backward(pair, sums):
            sums = list(sums)
            for half in range(2):
                k = 2 * pair + half
                for a in (-1, 0, 1):
                    value = responses[k, (1 - a) * wide : (1 - a) * wide + own_rows, :]
                    for spot, number in enumerate(chosen):
                        sums[spot] = sums[spot] + filters[k, (a + 1) * 9 + number] * value
            return tuple(sums)

        sums = lax.fori_loop(
            0, channels // 2, backward, tuple(jnp.zeros((own_rows, LANES), jnp.float32) for _ in chosen)
        )
        for spot, number in enumerate(chosen):
            b, e = lateral_taps[number]
            result = result + lateral_shift(rolled, sums[spot], -b, -e, half_y)
    joined[...] = result
    for j in range(tiles):
        prior_out[j] = joined[pl.ds(1 + j, coarse_rows, stride=wide), :]

    level = cells[...] // (width_x * width_y) - depth * rows
    inside = (level >= 0) & (level < rows)
    place_y = lax.broadcasted_iota(jnp.int32, (width_y, cells.shape[1]), 0)
    picked = (place_y == cells[...] % width_y) & inside
    for moment in range(lines.shape[0]):
        turned = jnp.where(picked, lines[moment].T, 0.0)
        trace_out[moment : moment + 1, :] = jnp.sum(turned, axis=0, keepdims=True)


def xor_pairs(count, bit):
    return [(i, i ^ bit) for i in range(count)]


def main(
    wave_prev, wave_now, adjoint, coarse_velocity, filters, wavelet, source_cell, receiver_cells
):
    f32 = jnp.float32
    steps, rows, width_x, width_y = adjoint.shape[1:]
    shots = lax.axis_size("shot")
    coarse_rows, columns = coarse_velocity.shape
    tiles = columns // LANES
    receiver_count = receiver_cells.shape[1]
    assert lax.axis_size("depth") == 2 and shots & (shots - 1) == 0 and shots > 1
    assert width_y == LANES and width_x % 64 == 0 and tiles * LANES == columns
    assert rows % 4 == 0 and rows >= REACH * steps and coarse_rows * 2 == rows and coarse_rows % 8 == 0
    assert receiver_count % 8 == 0 and filters.shape[0] % 4 == 0

    smem = pl.BlockSpec(memory_space=pltpu.SMEM)
    vmem = pl.BlockSpec(memory_space=pltpu.VMEM)
    hbm = pl.BlockSpec(memory_space=pltpu.HBM)
    anywhere = pl.BlockSpec(memory_space=pl.ANY)

    def shape_of(*extent):
        return jax.ShapeDtypeStruct(extent, f32)

    def scratch(*extent):
        return pltpu.VMEM(extent, f32)

    def in_hbm(value):
        return pltpu.with_memory_space_constraint(value, pltpu.HBM)

    def cost(cycles):
        return pl.CostEstimate(flops=cycles * 4096, bytes_accessed=cycles * 1024, transcendentals=0)

    shot, depth = lax.axis_index("shot"), lax.axis_index("depth")
    place = jnp.stack([shot, depth]).astype(jnp.int32)
    plane_size = width_x * width_y
    receivers = jnp.concatenate(
        [
            jnp.clip(receiver_cells // plane_size - depth * rows, 0, rows - 1),
            receiver_cells % plane_size // width_y,
        ]
    )
    swap = [(0, 1), (1, 0)]
    now_own, prev_own, adjoint_own = in_hbm(wave_now[0]), in_hbm(wave_prev[0]), in_hbm(adjoint[0])
    now_other = in_hbm(lax.ppermute(wave_now, "depth", swap)[0])
    prev_other = in_hbm(lax.ppermute(wave_prev, "depth", swap)[0])
    extent = REACH * (steps - 1)

    raw_block = coarse_velocity.reshape(coarse_rows, tiles, LANES).transpose(1, 0, 2)
    inside = rows - REACH
    laplace_in, base_in, block = pl.pallas_call(
        inner_kernel,
        out_shape=(shape_of(inside, width_x, width_y),) * 2 + (shape_of(tiles, coarse_rows, LANES),),
        in_specs=[smem, hbm, hbm, hbm],
        out_specs=(vmem, vmem, vmem),
        scratch_shapes=[
            scratch(rows + 2 * REACH, width_x + 2 * PAD, width_y), scratch(inside, width_x, width_y),
            pltpu.SemaphoreType.DMA((rows // 4,)), pltpu.SemaphoreType.DMA((rows // 4,)),
        ],
        cost_estimate=cost(2000),
        compiler_params=pltpu.CompilerParams(vmem_limit_bytes=GRANT),
        name="inner",
    )(place, now_own, prev_own, in_hbm(raw_block))
    laplace_beyond, base_beyond = pl.pallas_call(
        outer_kernel,
        out_shape=(shape_of(REACH + extent, width_x, width_y),) * 2,
        in_specs=[smem] + [hbm] * 4,
        out_specs=(vmem, vmem),
        scratch_shapes=[
            scratch(rows + 2 * REACH, width_x + 2 * PAD, width_y), scratch(REACH + extent, width_x, width_y),
            pltpu.SemaphoreType.DMA((rows // 4 + 1,)), pltpu.SemaphoreType.DMA((2,)),
        ],
        cost_estimate=cost(2500),
        compiler_params=pltpu.CompilerParams(vmem_limit_bytes=GRANT),
        name="outer",
    )(place, now_own, now_other, prev_own, prev_other)

    def hop(value, bit):
        return lax.ppermute(value, "shot", xor_pairs(shots, bit))

    bit = 1
    near = hop(raw_block[None], bit)
    near = jnp.concatenate([block[None], near], axis=0)
    while 4 * bit < shots:
        bit *= 2
        near = jnp.concatenate([near, hop(near, bit)], axis=0)
    bit *= 2
    far = hop(near, bit)
    other_near = lax.ppermute(near, "depth", swap)
    other_far = lax.ppermute(far, "depth", swap)

    all_rows = shots * tiles * coarse_rows
    image, lines, prev_out, now_out = pl.pallas_call(
        wave_kernel,
        out_shape=(
            shape_of(shots, tiles, coarse_rows, LANES), shape_of(steps, receiver_count, width_y),
            shape_of(rows, width_x, width_y), shape_of(rows, width_x, width_y),
        ),
        in_specs=[smem] * 4 + [vmem] * 8 + [hbm] * 3,
        out_specs=(vmem, vmem, hbm, hbm),
        scratch_shapes=[
            scratch(steps - 1, 2 * rows + 2 * REACH, width_x + 2 * PAD, width_y),
            scratch(steps, rows, width_x, width_y),
            scratch(rows, width_x, width_y),
            scratch(rows + extent, width_x, width_y),
            scratch(2 * coarse_rows, width_x, width_y),
            scratch(all_rows, LANES),
            scratch(all_rows, LANES),
            scratch(rows, width_x, width_y),
            scratch(width_x, width_y),
            pltpu.SemaphoreType.DMA((4 + steps,)),
        ],
        cost_estimate=cost(13000),
        compiler_params=pltpu.CompilerParams(vmem_limit_bytes=GRANT),
        name="wave",
    )(
        place, source_cell, wavelet, receivers, near, far, other_near, other_far,
        laplace_in, base_in, laplace_beyond, base_beyond, now_own, now_other, adjoint_own,
    )

    wide = tiles + 2
    total_rows = (coarse_rows + 4) * wide
    height = -(-total_rows // 8) * 8 + 8
    response_rows = -(-(coarse_rows + 2) * wide // 8) * 8
    channels = filters.shape[0]
    responses = pl.pallas_call(
        response_kernel,
        out_shape=shape_of(channels, response_rows, LANES),
        in_specs=[smem, smem, vmem, vmem, vmem, vmem],
        out_specs=vmem,
        scratch_shapes=[scratch(height, LANES), scratch(height + 16, LANES), scratch(9, height, LANES)],
        cost_estimate=cost(2600),
        compiler_params=pltpu.CompilerParams(vmem_limit_bytes=4 * 1024 * 1024),
        name="response",
    )(place, filters, near, far, other_near, other_far)
    prior, trace = pl.pallas_call(
        functools.partial(prior_kernel, (rows, width_x, width_y, coarse_rows, tiles)),
        out_shape=(shape_of(tiles, coarse_rows, LANES), shape_of(steps, receiver_count)),
        in_specs=[smem, smem, vmem, vmem, vmem],
        out_specs=(vmem, vmem),
        scratch_shapes=[scratch(coarse_rows * wide, LANES), scratch(coarse_rows * wide + 16, LANES)],
        cost_estimate=cost(2000),
        compiler_params=pltpu.CompilerParams(vmem_limit_bytes=4 * 1024 * 1024),
        name="prior",
    )(place, filters, responses, receiver_cells, lines)

    trace_other = lax.ppermute(trace, "depth", swap)
    kept = image
    while bit > 0:
        arrived = hop(kept[bit:], bit)
        kept = kept[:bit] + arrived
        bit //= 2
    share = kept[0] * ((-2.0 * courant * courant / SCALE) / block) + prior
    gradient = share.transpose(1, 0, 2).reshape(coarse_rows, columns)
    return gradient, prev_out[None], now_out[None], (trace + trace_other)[None]


def solution(mesh):
    return jax.shard_map(
        main,
        mesh=mesh,
        in_specs=(
            P(("grp", "shot"), "depth", None, None),
            P(("grp", "shot"), "depth", None, None),
            P(("grp", "shot"), None, "depth", None, None),
            P(("grp", "depth"), "shot"),
            P(),
            P(("grp", "shot"), None),
            P(("grp", "shot")),
            P(("grp", "shot"), None),
        ),
        out_specs=(
            P(("grp", "depth"), "shot"),
            P(("grp", "shot"), "depth", None, None),
            P(("grp", "shot"), "depth", None, None),
            P(("grp", "shot"), None, None),
        ),
        check_vma=False,
    )
```

```python
import functools

import jax
import jax.numpy as jnp
from jax import lax
from jax.experimental import pallas as pl
from jax.experimental.pallas import tpu as pltpu
from jax.sharding import PartitionSpec as P


SCALE = 5040.0
CENTRE = -3.0 * 14350.0
WEIGHTS = (8064.0, -1008.0, 128.0, -9.0)
REACH = 4
PAD = 8
LANES = 128
TILE = 16
GRANT = 32 * 1024 * 1024
courant = 0.1
lateral_taps = [(b, e) for b in (-1, 0, 1) for e in (-1, 0, 1)]


def split(value):
    high = value.astype(jnp.bfloat16)
    low = (value - high.astype(jnp.float32)).astype(jnp.bfloat16)
    return jnp.concatenate([high, low], axis=1)


def banded(width):
    row = lax.broadcasted_iota(jnp.int32, (width, width), 0)
    column = lax.broadcasted_iota(jnp.int32, (width, width), 1)
    distance = jnp.abs(row - column)
    result = jnp.zeros((width, width), jnp.float32)
    for reach in range(1, REACH + 1):
        result = jnp.where(distance == reach, WEIGHTS[reach - 1], result)
    return jnp.concatenate([result, result], axis=0).astype(jnp.bfloat16)


def spreading(half):
    row = lax.broadcasted_iota(jnp.int32, (LANES, 2 * LANES), 0)
    column = lax.broadcasted_iota(jnp.int32, (LANES, 2 * LANES), 1)
    wanted = jnp.where(column < LANES, column // 2, half + (column - LANES) // 2)
    result = jnp.where(row == wanted, 1.0, 0.0)
    return jnp.concatenate([result, result], axis=0).astype(jnp.bfloat16)


def pairing(offset):
    row = lax.broadcasted_iota(jnp.int32, (LANES, LANES), 0)
    column = lax.broadcasted_iota(jnp.int32, (LANES, LANES), 1)
    result = jnp.where(row // 2 + offset == column, 1.0, 0.0)
    return jnp.concatenate([result, result], axis=0).astype(jnp.bfloat16)


def find(cell, width_x, width_y):
    line = quotient(cell, width_y)
    plane = quotient(line, width_x)
    return plane, line - plane * width_x, cell - line * width_y


def stencil_group(planes, first, x, band, use):
    stacked = jnp.concatenate([planes[first + REACH + i, x : x + TILE, :] for i in range(4)], axis=0)
    along_y = jnp.dot(split(stacked), band, preferred_element_type=jnp.float32)
    column = [planes[first + i, x : x + TILE, :] for i in range(4 + 2 * REACH)]
    for i in range(4):
        centre = column[REACH + i]
        total = CENTRE * centre + along_y[i * TILE : (i + 1) * TILE]
        for reach in range(1, REACH + 1):
            pairs = (column[REACH + i + reach] + column[REACH + i - reach]) + (
                planes[first + REACH + i, x + reach : x + reach + TILE, :]
                + planes[first + REACH + i, x - reach : x - reach + TILE, :]
            )
            total = total + WEIGHTS[reach - 1] * pairs
        use(i, slice(x - PAD, x - PAD + TILE), centre, total)


def clear_sides(planes, count, width_x, width_y):
    def step(index, carry):
        for offset in range(4):
            planes[4 * index + offset, 0:PAD, :] = jnp.zeros((PAD, width_y), jnp.float32)
            planes[4 * index + offset, PAD + width_x : 2 * PAD + width_x, :] = jnp.zeros((PAD, width_y), jnp.float32)
        return carry

    assert count % 4 == 0
    lax.fori_loop(0, count // 4, step, 0)


def first_steps(planes, laplace, base, offset, target, earlier, earlier_first, band):
    for part in range((planes.shape[1] - 2 * PAD) // TILE):

        def use(i, inner, centre, total):
            laplace[target + i, inner, :] = total
            base[target + i, inner, :] = 2.0 * centre - earlier[earlier_first + i, inner, :]

        stencil_group(planes, offset, PAD + part * TILE, band, use)


def first_kernel(first_group, groups, place, ahead, now_own, now_other, prev_own, prev_other, *others):
    del ahead
    if len(others) == 8:
        block, laplace, base, block_out, planes, earlier, field_sems, sems = others
        block_copy = pltpu.make_async_copy(block, block_out, sems.at[groups])
        block_copy.start()
    else:
        laplace, base, planes, earlier, field_sems, sems = others
        block_copy = None
    depth = place[1]
    rows, width_x, width_y = now_own.shape
    chunks = groups + 2

    def turned(index, count):
        return index + depth * (count - 1 - 2 * index)

    def source_rows(number, own, other):
        if number < 1:
            return own.at[pl.ds(4 * turned(rows // 4 - 1 + number, rows // 4), 4)]
        return other.at[pl.ds(4 * turned(number - 1, rows // 4), 4)]

    outside = [chunk for chunk in range(chunks) if first_group - 1 + chunk <= -(rows // 4)]
    fields = {
        chunk: pltpu.make_async_copy(
            source_rows(first_group - 1 + chunk, now_own, now_other),
            planes.at[pl.ds(4 * turned(chunk, chunks), 4), pl.ds(PAD, width_x)], field_sems.at[chunk],
        )
        for chunk in range(chunks) if chunk not in outside
    }
    befores = [
        pltpu.make_async_copy(
            source_rows(first_group + index, prev_own, prev_other), earlier.at[pl.ds(4 * turned(index, groups), 4)],
            sems.at[index],
        )
        for index in range(groups)
    ]
    order = list(fields.values())
    for copy in (*order[: 3 - len(outside)], befores[0], *order[3 - len(outside) :], *befores[1:]):
        copy.start()
    clear_sides(planes, 4 * chunks, width_x, width_y)
    for chunk in outside:
        for i in range(4):
            planes[4 * turned(chunk, chunks) + i] = jnp.zeros((width_x + 2 * PAD, width_y), jnp.float32)
    band = banded(width_y)
    for chunk in range(2):
        if chunk in fields:
            fields[chunk].wait()

    def group(index, carry):
        pltpu.make_async_copy(
            now_own.at[pl.ds(0, 4)], planes.at[pl.ds(0, 4), pl.ds(PAD, width_x)], field_sems.at[index + 2]
        ).wait()
        pltpu.make_async_copy(prev_own.at[pl.ds(0, 4)], earlier.at[pl.ds(0, 4)], sems.at[index]).wait()
        target = 4 * turned(index, groups)
        first_steps(planes, laplace, base, target, target, earlier, target, band)
        return carry

    lax.fori_loop(0, groups, group, 0)
    if block_copy is not None:
        block_copy.wait()


def wave_kernel(
    place, source, pulses, near, far, other_near, other_far,
    laplace_in, base_in, laplace_edge, base_edge, laplace_beyond, base_beyond, now_other, now_own, adjoint,
    image_out, *outputs_and_scratch,
):
    shot, depth = place[0], place[1]
    steps, rows, width_x, width_y = adjoint.shape
    levels_out = outputs_and_scratch[:steps]
    adjoints, last, start, speed, even_rows, odd_rows, imaging, pair_sum, sems = outputs_and_scratch[
        steps : steps + 9
    ]
    fields = outputs_and_scratch[steps + 9 :]
    half_x, half_y = width_x // 2, width_y // 2
    blocks, tiles, coarse_rows = 2 * near.shape[0], near.shape[1], near.shape[2]
    half_blocks = near.shape[0]
    own_start = depth * rows

    extent = REACH * (steps - 1)
    starts = [pltpu.make_async_copy(now_own, start, sems.at[steps])]
    incoming = [
        pltpu.make_async_copy(adjoint.at[moment], adjoints.at[moment], sems.at[moment]) for moment in range(steps)
    ]
    for copy in (incoming[0], *starts, *incoming[1:]):
        copy.start()

    edge = depth * (2 * rows + REACH)
    for level in range(steps - 1):
        clear_sides(fields[level], 2 * rows + 2 * REACH, width_x, width_y)

    def clear_edge(z, carry):
        for level in range(steps - 1):
            fields[level][edge + z] = jnp.zeros((width_x + 2 * PAD, width_y), jnp.float32)
        return carry

    lax.fori_loop(0, REACH, clear_edge, 0)

    spread = spreading(half_y)
    group = tiles * coarse_rows
    lines = half_x // 2
    for parts, slab in (((near, far), depth), ((other_near, other_far), 1 - depth)):
        for part_number, part in enumerate(parts):
            flat = part[...].reshape(half_blocks * group, LANES)
            fine = jnp.dot(split(flat), spread, preferred_element_type=jnp.float32)
            fine = courant * fine
            fine = fine * fine * (1.0 / SCALE)
            for position in range(half_blocks):
                target = (shot ^ mirrored(position + part_number * half_blocks, blocks)) * group
                here = pl.ds(pl.multiple_of(target, group), group)
                even_rows[here, :] = fine[position * group : (position + 1) * group, :LANES]
                odd_rows[here, :] = fine[position * group : (position + 1) * group, LANES:]
        for row in range(coarse_rows):
            even = even_rows[pl.ds(row, lines, stride=coarse_rows), :]
            odd = odd_rows[pl.ds(row, lines, stride=coarse_rows), :]
            plane = slab * coarse_rows + row
            speed[plane, pl.ds(0, lines, stride=4), :] = even
            speed[plane, pl.ds(1, lines, stride=4), :] = even
            speed[plane, pl.ds(2, lines, stride=4), :] = odd
            speed[plane, pl.ds(3, lines, stride=4), :] = odd

    band = banded(width_y)
    outgoing = [
        pltpu.make_async_copy(
            fields[level].at[pl.ds(REACH + own_start, rows), pl.ds(PAD, width_x)], levels_out[level],
            sems.at[steps + 2 + level],
        )
        for level in range(steps - 1)
    ]
    outgoing.append(pltpu.make_async_copy(last, levels_out[steps - 1], sems.at[2 * steps + 1]))

    source_z, source_x, source_y = find(source[0], width_x, width_y)
    source_mask = lax.broadcasted_iota(jnp.int32, (1, width_y), 1) == source_y
    for moment in range(steps):
        extra = REACH * (steps - 1 - moment)
        level = moment - 1

        def advance(z0, own):
            half = quotient(z0, 2)
            for part in range(width_x // TILE):

                def use(i, inner, centre, total):
                    z = z0 + i
                    wide = slice(inner.start + PAD, inner.stop + PAD)
                    if moment == 1:
                        before = (start if own else now_other)[z - (own_start if own else rows - own_start), inner, :]
                    else:
                        before = fields[level - 1][z + REACH, wide, :]
                    following = 2.0 * centre - before + speed[half + i // 2, inner, :] * total
                    if moment + 1 < steps:
                        fields[level + 1][z + REACH, wide, :] = following
                    else:
                        last[z - own_start, inner, :] = following
                    if own:
                        own_z = z - own_start
                        imaging[own_z, inner, :] += adjoints[moment, own_z, inner, :] * total

                stencil_group(fields[level], z0, PAD + part * TILE, band, use)

        amount = SCALE * pulses[0, moment]

        def add_source(low, count):
            @pl.when((source_z >= low) & (source_z < low + count))
            def _():
                bump = jnp.where(source_mask, speed[source_z // 2, pl.ds(source_x, 1), :] * amount, 0.0)
                if moment + 1 < steps:
                    fields[moment][source_z + REACH, pl.ds(source_x + PAD, 1), :] += bump
                else:
                    last[source_z - own_start, pl.ds(source_x, 1), :] += bump

        if moment == 0:

            def begin(first, laplace, base, offset, own):
                def pair(index, carry):
                    z = first + 2 * index
                    half = quotient(z, 2)
                    for part in range(width_x // TILE):
                        inner = slice(part * TILE, (part + 1) * TILE)
                        wide = slice(inner.start + PAD, inner.stop + PAD)
                        factor = speed[half, inner, :]
                        for i in range(2):
                            row = offset + 2 * index + i
                            total = laplace[row, inner, :]
                            fields[0][z + i + REACH, wide, :] = base[row, inner, :] + factor * total
                            if own:
                                own_z = z + i - own_start
                                imaging[own_z, inner, :] = adjoints[0, own_z, inner, :] * total
                    return carry

                return pair

            inside = rows - REACH
            edge_other = begin(inside + (1 - depth) * REACH, laplace_edge, base_edge, (1 - depth) * REACH, False)
            lax.fori_loop(0, REACH // 2, edge_other, 0)
            beyond_start = (1 - depth) * (rows + REACH) + depth * (rows - extent)
            lax.fori_loop(0, (extent - REACH) // 2, begin(beyond_start, laplace_beyond, base_beyond, 0, False), 0)
            incoming[0].wait()
            lax.fori_loop(0, inside // 2, begin(own_start + depth * REACH, laplace_in, base_in, 0, True), 0)
            edge_own = begin(own_start + (1 - depth) * inside, laplace_edge, base_edge, depth * REACH, True)
            lax.fori_loop(0, REACH // 2, edge_own, 0)
        else:
            incoming[moment].wait()
            if moment == 1:
                for copy in starts:
                    copy.wait()

            def own_group(index, carry):
                advance(own_start + 4 * index, True)
                if moment + 1 == steps:
                    add_source(own_start + 4 * index, 4)
                    pltpu.make_async_copy(
                        last.at[pl.ds(4 * index, 4)], levels_out[moment].at[pl.ds(4 * index, 4)], sems.at[2 * steps + 1]
                    ).start()
                return carry

            def other_group(index, carry):
                advance(jnp.where(depth == 0, rows, rows - extra) + 4 * index, False)
                return carry

            lax.fori_loop(0, rows // 4, own_group, 0)
            if extra > 0:
                lax.fori_loop(0, extra // 4, other_group, 0)

        if moment + 1 < steps:
            add_source(own_start - depth * extra, rows + extra)

        @pl.when((source_z >= own_start) & (source_z < own_start + rows))
        def _():
            own_z = source_z - own_start
            weight = adjoints[moment, own_z, pl.ds(source_x, 1), :] * amount
            imaging[own_z, pl.ds(source_x, 1), :] += jnp.where(source_mask, weight, 0.0)

        if moment + 1 < steps:
            outgoing[moment].start()

    gather = jnp.concatenate([pairing(0), pairing(half_y)], axis=0)
    for row in range(coarse_rows):
        pair_sum[...] = imaging[2 * row] + imaging[2 * row + 1]
        even = pair_sum[pl.ds(0, lines, stride=4), :] + pair_sum[pl.ds(1, lines, stride=4), :]
        odd = pair_sum[pl.ds(2, lines, stride=4), :] + pair_sum[pl.ds(3, lines, stride=4), :]
        coarse = jnp.dot(
            jnp.concatenate([split(even), split(odd)], axis=1), gather, preferred_element_type=jnp.float32
        )
        even_rows[pl.ds(row, lines, stride=coarse_rows), :] = coarse
    for position in range(blocks):
        origin = pl.ds(pl.multiple_of((shot ^ mirrored(position, blocks)) * group, group), group)
        image_out[position] = even_rows[origin, :].reshape(tiles, coarse_rows, LANES)

    for copy in outgoing:
        copy.wait()


def lateral_shift(rolled, value, b, e, half_y):
    lane = lax.broadcasted_iota(jnp.int32, (1, LANES), 1)
    column = lane % half_y
    count = value.shape[0]
    offset = b * half_y + e
    if offset == 0:
        return value
    turned = pltpu.roll(value, (-offset) % LANES, 1)
    rolled[8 : 8 + count, :] = turned
    if offset > 0:
        moved = jnp.where(lane < LANES - offset, turned, rolled[9 : 9 + count, :])
    else:
        moved = jnp.where(lane >= -offset, turned, rolled[7 : 7 + count, :])
    if e != 0:
        moved = jnp.where((column + e >= 0) & (column + e < half_y), moved, 0.0)
    return moved


def quotient(value, divisor):
    if divisor & (divisor - 1) == 0:
        return lax.shift_right_logical(value, divisor.bit_length() - 1)
    return lax.div(value, divisor)


def receiver_rows(extent, cells, depth, levels, planes, lookup, receivers, sems):
    rows, width_x, width_y = extent
    count = planes.shape[0]
    line = quotient(cells[...], width_y)
    plane = quotient(line, width_x)
    lookup[...] = line + (jnp.clip(plane - depth * rows, 0, rows - 1) - plane) * width_x
    copies = [pltpu.make_async_copy(levels[t], planes.at[t], sems.at[t]) for t in range(count)]
    copies.append(pltpu.make_async_copy(lookup, receivers, sems.at[count]))
    for copy in copies:
        copy.start()

    def take(lines):
        for copy in copies:
            copy.wait()

        def fetch(index, carry):
            for offset in range(8):
                number = index * 8 + offset
                row = receivers[0, number]
                for moment in range(count):
                    lines[moment, pl.ds(number, 1), :] = planes[moment, pl.ds(row, 1), :]
            return carry

        lax.fori_loop(0, receivers.shape[1] // 8, fetch, 0)

    return take


def response_kernel(
    extent, early, place, filters, cells, near, far, other_near, other_far, *others
):
    shot, depth = place[0], place[1]
    levels = others[:early]
    responses, lines, joined, rolled, shifts, *reading = others[early:]
    take = receiver_rows(extent, cells, depth, levels, *reading)
    half_blocks, tiles, coarse_rows = near.shape[0], near.shape[1], near.shape[2]
    shots = 2 * half_blocks
    half_y = LANES // 2
    channels = filters.shape[0]
    wide = tiles + 2
    total_tiles = shots * tiles
    inner_rows = (coarse_rows + 2) * wide
    padded_rows = responses.shape[1]

    joined[...] = jnp.zeros_like(joined)
    rolled[...] = jnp.zeros_like(rolled)
    for j in range(wide):
        absolute = shot * tiles - 1 + j
        exists = (absolute >= 0) & (absolute < total_tiles)
        safe = jnp.clip(absolute, 0, total_tiles - 1)
        owner = quotient(safe, tiles)
        position = mirrored(shot ^ owner, shots)
        which = safe - owner * tiles
        for own_part, other_part, chosen, start in (
            (near, other_near, position < half_blocks, 0), (far, other_far, position >= half_blocks, half_blocks)
        ):

            @pl.when(exists & chosen)
            def _():
                joined[pl.ds(2 * wide + j, coarse_rows, stride=wide), :] = own_part[position - start, which]
                tile = other_part[position - start, which]

                @pl.when(depth == 1)
                def _():
                    joined[pl.ds(j, 1), :] = tile[coarse_rows - 2 : coarse_rows - 1]
                    joined[pl.ds(wide + j, 1), :] = tile[coarse_rows - 1 : coarse_rows]

                @pl.when(depth == 0)
                def _():
                    joined[pl.ds((coarse_rows + 2) * wide + j, 1), :] = tile[0:1]
                    joined[pl.ds((coarse_rows + 3) * wide + j, 1), :] = tile[1:2]

    whole = joined[...]
    for number, (b, e) in enumerate(lateral_taps):
        shifts[number] = lateral_shift(rolled, whole, b, e, half_y)

    row = lax.broadcasted_iota(jnp.int32, (padded_rows, LANES), 0)
    valid = row < inner_rows
    valid = valid & ((row >= wide) | (depth != 0))
    valid = valid & ((row < (coarse_rows + 1) * wide) | (depth != 1))
    first_tile = row == 0
    last_tile = row == wide - 1
    for z in range(1, coarse_rows + 2):
        first_tile = first_tile | (row == z * wide)
        last_tile = last_tile | (row == z * wide + wide - 1)
    valid = valid & jnp.logical_not(first_tile & (shot == 0))
    valid = valid & jnp.logical_not(last_tile & (shot == shots - 1))
    keep = jnp.where(valid, 1.0, 0.0)

    def forward(index, carry):
        scores = [jnp.zeros((padded_rows, LANES), jnp.float32) for _ in range(4)]
        for a in (-1, 0, 1):
            for number in range(9):
                value = shifts[number, (1 + a) * wide : (1 + a) * wide + padded_rows, :]
                tap = (a + 1) * 9 + number
                for k in range(4):
                    scores[k] = scores[k] + filters[index * 4 + k, tap] * value
        for k in range(4):
            answer = scores[k] / (1.0 + scores[k] * scores[k])
            responses[index * 4 + k] = jnp.where(keep > 0.0, answer, 0.0)
        return carry

    lax.fori_loop(0, channels // 4, forward, 0)
    take(lines)


def prior_kernel(
    shape, place, filters, responses, cells, *others
):
    late, rows, width_x, width_y, coarse_rows, tiles = shape
    levels = others[:late]
    early_lines, prior_out, trace_out, joined, rolled, lines, *reading = others[late:]
    depth = place[1]
    take = receiver_rows((rows, width_x, width_y), cells, depth, levels, *reading)
    half_y = LANES // 2
    channels = filters.shape[0]
    wide = tiles + 2
    own_rows = coarse_rows * wide
    rolled[...] = jnp.zeros_like(rolled)
    result = jnp.zeros((own_rows, LANES), jnp.float32)
    for chosen in ((0, 1, 2, 3, 4), (5, 6, 7, 8)):

        def backward(pair, sums):
            sums = list(sums)
            for half in range(2):
                k = 2 * pair + half
                for a in (-1, 0, 1):
                    value = responses[k, (1 - a) * wide : (1 - a) * wide + own_rows, :]
                    for spot, number in enumerate(chosen):
                        sums[spot] = sums[spot] + filters[k, (a + 1) * 9 + number] * value
            return tuple(sums)

        sums = lax.fori_loop(
            0, channels // 2, backward, tuple(jnp.zeros((own_rows, LANES), jnp.float32) for _ in chosen)
        )
        for spot, number in enumerate(chosen):
            b, e = lateral_taps[number]
            result = result + lateral_shift(rolled, sums[spot], -b, -e, half_y)
    joined[...] = result
    for j in range(tiles):
        prior_out[j] = joined[pl.ds(1 + j, coarse_rows, stride=wide), :]

    take(lines)
    level = cells[...] // (width_x * width_y) - depth * rows
    inside = (level >= 0) & (level < rows)
    place_y = lax.broadcasted_iota(jnp.int32, (width_y, cells.shape[1]), 0)
    picked = (place_y == cells[...] % width_y) & inside
    early = early_lines.shape[0]
    for moment in range(early + late):
        found = early_lines[moment] if moment < early else lines[moment - early]
        turned = jnp.where(picked, found.T, 0.0)
        trace_out[moment : moment + 1, :] = jnp.sum(turned, axis=0, keepdims=True)


def join_kernel(first, second, out):
    out[0 : first.shape[0]] = first[...]
    out[first.shape[0] :] = second[...]


def mirrored(value, count):
    bits = count.bit_length() - 1
    result = 0
    for bit in range(bits):
        result = result | (((value >> bit) & 1) << (bits - 1 - bit))
    return result


def xor_pairs(count, bit):
    return [(i, i ^ bit) for i in range(count)]


def main(
    wave_prev, wave_now, adjoint, coarse_velocity, filters, wavelet, source_cell, receiver_cells
):
    f32 = jnp.float32
    steps, rows, width_x, width_y = adjoint.shape[1:]
    shots = lax.axis_size("shot")
    coarse_rows, columns = coarse_velocity.shape
    tiles = columns // LANES
    receiver_count = receiver_cells.shape[1]
    assert lax.axis_size("depth") == 2 and shots & (shots - 1) == 0 and shots > 1
    assert width_y == LANES and width_x % 64 == 0 and tiles * LANES == columns
    assert rows % 4 == 0 and rows >= REACH * steps and coarse_rows * 2 == rows and coarse_rows % 8 == 0
    assert receiver_count % 8 == 0 and filters.shape[0] % 4 == 0

    smem = pl.BlockSpec(memory_space=pltpu.SMEM)
    vmem = pl.BlockSpec(memory_space=pltpu.VMEM)
    hbm = pl.BlockSpec(memory_space=pltpu.HBM)
    anywhere = pl.BlockSpec(memory_space=pl.ANY)

    def shape_of(*extent):
        return jax.ShapeDtypeStruct(extent, f32)

    def scratch(*extent):
        return pltpu.VMEM(extent, f32)

    def in_hbm(value):
        return pltpu.with_memory_space_constraint(value, pltpu.HBM)

    def cost(cycles):
        return pl.CostEstimate(flops=cycles * 4096, bytes_accessed=cycles * 1024, transcendentals=0)

    shot, depth = lax.axis_index("shot"), lax.axis_index("depth")
    place = jnp.stack([shot, depth]).astype(jnp.int32)
    swap = [(0, 1), (1, 0)]
    now_own, prev_own, adjoint_own = in_hbm(wave_now[0]), in_hbm(wave_prev[0]), in_hbm(adjoint[0])
    now_other = lax.ppermute(wave_now, "depth", swap)[0]
    prev_other = lax.ppermute(wave_prev, "depth", swap)[0]
    extent = REACH * (steps - 1)

    raw_block = coarse_velocity.reshape(coarse_rows, tiles, LANES).transpose(1, 0, 2)

    def first_step(first_group, groups, fields, ahead, block=None):
        shapes, specs = (shape_of(4 * groups, width_x, width_y),) * 2, [smem, smem, hbm, anywhere, hbm, anywhere]
        if block is not None:
            shapes, specs = (*shapes, shape_of(*block.shape)), [*specs, hbm]
            fields = (*fields, in_hbm(block))
        return pl.pallas_call(
            functools.partial(first_kernel, first_group, groups),
            out_shape=shapes,
            in_specs=specs,
            out_specs=(vmem,) * len(shapes),
            scratch_shapes=[
                scratch(4 * groups + 2 * REACH, width_x + 2 * PAD, width_y), scratch(4 * groups, width_x, width_y),
                pltpu.SemaphoreType.DMA((groups + 2,)), pltpu.SemaphoreType.DMA((groups + 1,)),
            ],
            cost_estimate=cost(700 * groups),
            compiler_params=pltpu.CompilerParams(vmem_limit_bytes=GRANT),
        )(place, ahead, *fields)

    slab_groups = rows // 4
    everywhere = (now_own, now_other, prev_own, prev_other)
    laplace_in, base_in, block = first_step(
        1 - slab_groups, slab_groups - 1, (now_own, now_own, prev_own, prev_own), place, raw_block
    )
    laplace_edge, base_edge = first_step(0, 2, everywhere, place)
    laplace_beyond, base_beyond = first_step(2, extent // 4 - 1, everywhere, source_cell)

    def join(first, second):
        return pl.pallas_call(
            join_kernel,
            out_shape=shape_of(2 * first.shape[0], *first.shape[1:]),
            in_specs=[vmem, vmem],
            out_specs=vmem,
            compiler_params=pltpu.CompilerParams(vmem_limit_bytes=2 * 1024 * 1024),
            name="join",
        )(first, second)

    def hop(value, bit):
        return lax.ppermute(value, "shot", xor_pairs(shots, mirrored(bit, shots)))

    bit = 1
    near = hop(raw_block[None], bit)
    near = join(block[None], near)
    while 4 * bit < shots:
        bit *= 2
        near = join(near, hop(near, bit))
    bit *= 2
    far = hop(near, bit)
    other_near = lax.ppermute(near, "depth", swap)
    other_far = lax.ppermute(far, "depth", swap)

    all_rows = shots * tiles * coarse_rows
    image, *levels = pl.pallas_call(
        wave_kernel,
        out_shape=(
            shape_of(shots, tiles, coarse_rows, LANES), *[pltpu.HBM((rows, width_x, width_y), f32)] * steps,
        ),
        in_specs=[smem, smem, smem] + [vmem] * 11 + [hbm] * 2,
        out_specs=(vmem, *[hbm] * steps),
        scratch_shapes=[
            scratch(steps, rows, width_x, width_y),
            scratch(rows, width_x, width_y),
            scratch(rows, width_x, width_y),
            scratch(2 * coarse_rows, width_x, width_y),
            scratch(all_rows, LANES),
            scratch(all_rows, LANES),
            scratch(rows, width_x, width_y),
            scratch(width_x, width_y),
            pltpu.SemaphoreType.DMA((2 + 2 * steps,)),
        ]
        + [scratch(2 * rows + 2 * REACH, width_x + 2 * PAD, width_y)] * (steps - 1),
        cost_estimate=cost(13000),
        compiler_params=pltpu.CompilerParams(vmem_limit_bytes=GRANT),
        name="wave",
    )(
        place, source_cell, wavelet, near, far, other_near, other_far,
        laplace_in, base_in, laplace_edge, base_edge, laplace_beyond, base_beyond, now_other, now_own, adjoint_own,
    )

    wide = tiles + 2
    total_rows = (coarse_rows + 4) * wide
    height = -(-total_rows // 8) * 8 + 8
    response_rows = -(-(coarse_rows + 2) * wide // 8) * 8
    channels = filters.shape[0]
    early = steps // 2

    flat = [in_hbm(level.reshape(rows * width_x, width_y)) for level in levels]

    def reading(count):
        return [
            scratch(count, rows * width_x, width_y), pltpu.VMEM((1, receiver_count), jnp.int32),
            pltpu.SMEM((1, receiver_count), jnp.int32), pltpu.SemaphoreType.DMA((count + 1,)),
        ]

    responses, lines = pl.pallas_call(
        functools.partial(response_kernel, (rows, width_x, width_y), early),
        out_shape=(shape_of(channels, response_rows, LANES), shape_of(early, receiver_count, width_y)),
        in_specs=[smem, smem, vmem, vmem, vmem, vmem, vmem] + [hbm] * early,
        out_specs=(vmem, vmem),
        scratch_shapes=[
            scratch(height, LANES), scratch(height + 16, LANES), scratch(9, height, LANES), *reading(early)
        ],
        cost_estimate=cost(2600),
        compiler_params=pltpu.CompilerParams(vmem_limit_bytes=8 * 1024 * 1024),
        name="response",
    )(place, filters, receiver_cells, near, far, other_near, other_far, *flat[:early])
    late = steps - early
    prior, trace = pl.pallas_call(
        functools.partial(prior_kernel, (late, rows, width_x, width_y, coarse_rows, tiles)),
        out_shape=(shape_of(tiles, coarse_rows, LANES), shape_of(steps, receiver_count)),
        in_specs=[smem, smem, vmem, vmem] + [hbm] * late + [vmem],
        out_specs=(vmem, vmem),
        scratch_shapes=[
            scratch(coarse_rows * wide, LANES), scratch(coarse_rows * wide + 16, LANES),
            scratch(late, receiver_count, width_y), *reading(late),
        ],
        cost_estimate=cost(2600),
        compiler_params=pltpu.CompilerParams(vmem_limit_bytes=8 * 1024 * 1024),
        name="prior",
    )(place, filters, responses, receiver_cells, *flat[early:], lines)

    trace_other = lax.ppermute(trace, "depth", swap)
    kept = image
    while bit > 0:
        arrived = hop(kept[bit:], bit)
        kept = kept[:bit] + arrived
        bit //= 2
    share = kept[0] * ((-2.0 * courant * courant / SCALE) / block) + prior
    gradient = share.transpose(1, 0, 2).reshape(coarse_rows, columns)
    return gradient, levels[-2][None], levels[-1][None], (trace + trace_other)[None]


def solution(mesh):
    return jax.shard_map(
        main,
        mesh=mesh,
        in_specs=(
            P(("grp", "shot"), "depth", None, None),
            P(("grp", "shot"), "depth", None, None),
            P(("grp", "shot"), None, "depth", None, None),
            P(("grp", "depth"), "shot"),
            P(),
            P(("grp", "shot"), None),
            P(("grp", "shot")),
            P(("grp", "shot"), None),
        ),
        out_specs=(
            P(("grp", "depth"), "shot"),
            P(("grp", "shot"), "depth", None, None),
            P(("grp", "shot"), "depth", None, None),
            P(("grp", "shot"), None, None),
        ),
        check_vma=False,
    )
```
